32 devices in a mesh: pipe: 4 (over z), dp: 8 (over y, x, core).
Axes of the slice: x: 2, y: 2, z: 4, core: 2. Of those that a mesh axis runs over, the one named last changes fastest.
Arguments:
- saved: bfloat16 [2, 4, 1024, 4096], P(None, 'pipe', 'dp'), may hold values from -6 to 6
- grad_out: bfloat16 [1024, 4096], P('dp'), may hold values from -6 to 6
- gain: float32 [2, 4, 4096], P(None, 'pipe'), may hold values from 0.5 to 1.5
- w_value: bfloat16 [4, 4096, 512], P('pipe', 'dp'), may hold values from -0.09375 to 0.09375
Outputs:
- grad_x: bfloat16 [2, 4, 1024, 4096], P(None, 'pipe', 'dp')
- grad_w: float32 [4, 4096, 512], P('pipe', 'dp')
The draws below stay inside these ranges and needn't reach their ends.
All inputs are finite; a program needn't handle non-finite values.
Results may differ from the reference program's by a relative error of at most 0.012.
Values may be sent and summed in bfloat16 or wider, within the bound.
A program may use at most 64 MiB of HBM per device.

```python
import jax
import jax.numpy as jnp
from jax import lax

HEAD = 128
Q_HEADS = 32
KV_HEADS = 4
D = 4096
KV = 512
TOKENS = 1024
N_PIPE = 4


def spiked(entries, own_key, source, target, blocks, factor):
    owner, partner = [(jnp.arange(entries.shape[position]) // (entries.shape[position] // blocks)).reshape([-1 if axis == position else 1 for axis in range(entries.ndim)]) for position in (source, target)]
    chosen = jax.random.permutation(own_key, blocks)[partner]
    strong = (owner == chosen) | (owner == (partner + blocks // 2) % blocks)
    return jnp.where(strong, factor * entries, entries)


def block_scale(stream_key, extent, split, low, top_value):
    loudness = 1.0
    for position, shards_of in split:
        draws = jax.random.uniform(jax.random.fold_in(jax.random.fold_in(stream_key, 6), position), (shards_of,), jnp.float32, low / len(split), top_value / len(split))
        loudness = loudness * jnp.repeat(jnp.exp(draws), extent[position] // shards_of).reshape((-1,) + (1,) * (len(extent) - 1 - position))
    return loudness


def gaussian(key, dims, deviation, reach, shards=(), dtype=jnp.bfloat16):
    entries = deviation * jax.random.normal(key, dims, jnp.float32)
    if shards:
        entries = entries * block_scale(key, dims, shards, -0.22, 0.18)
    return jnp.clip(entries, -reach, reach).astype(dtype)


def noise_with(rng, shape, deviation, reach, pieces, heavy, kind=jnp.bfloat16):
    values = deviation * jax.random.normal(rng, shape, jnp.float32)
    if pieces:
        values = values * block_scale(rng, shape, pieces, -0.22, 0.18)
    return jnp.clip(spiked(values, jax.random.fold_in(rng, 3), *heavy), -reach, reach).astype(kind)


def setup_inputs(seed: int = 0) -> dict:
    arg_keys = jax.random.split(jax.random.key(seed), 5)
    saved = noise_with(arg_keys[0], (2, N_PIPE, TOKENS, D), 1.0, 6.0, ((1, 4), (2, 8)), (2, 3, 8, 2.0))
    grad_out = gaussian(arg_keys[1], (TOKENS, D), 1.0, 6.0, ((0, 8),))
    gain = jnp.clip(1.0 + 0.1 * jax.random.normal(arg_keys[2], (2, N_PIPE, D), jnp.float32), 0.5, 1.5)
    w_value = gaussian(arg_keys[3], (N_PIPE, D, KV), D ** -0.5, 0.09375, ((0, 4), (1, 8)))
    return {"saved": saved, "grad_out": grad_out, "gain": gain, "w_value": w_value}


def section_back(x, dy, g, w_mat):
    x32 = x.astype(jnp.float32)
    rinv = lax.rsqrt(lax.optimization_barrier(jnp.mean(x32 * x32, axis=-1, keepdims=True)) + 1e-05)
    normed = x32 * rinv
    hidden = (normed * g).astype(jnp.bfloat16)
    rows = x.shape[0]
    dv = dy.astype(jnp.float32).reshape(rows, KV_HEADS, Q_HEADS // KV_HEADS, HEAD).sum(2)
    dv = dv.reshape(rows, KV_HEADS * HEAD).astype(jnp.bfloat16)
    dh = lax.dot_general(dv, w_mat, (((1,), (1,)), ((), ())), preferred_element_type=jnp.float32)
    dhg = dh * g
    dx = dy.astype(jnp.float32) + rinv * (dhg - normed * lax.optimization_barrier(jnp.mean(dhg * normed, axis=-1, keepdims=True)))
    dx = dx.astype(jnp.bfloat16)
    gw = lax.dot_general(hidden, dv, (((0,), (0,)), ((), ())), preferred_element_type=jnp.float32)
    return (dx, gw)

def reference(saved, grad_out, gain, w_value):
    dy = grad_out
    grads_x = {}
    grads_w = {}
    for section in range(2 * N_PIPE - 1, -1, -1):
        loop_id = section // N_PIPE
        pair = section % N_PIPE
        dx, gw = section_back(saved[loop_id, pair], dy, gain[loop_id, pair], w_value[pair])
        grads_x[loop_id, pair] = dx
        grads_w[pair] = gw if loop_id == 1 else grads_w[pair] + gw
        dy = dx
    grad_x = jnp.stack([jnp.stack([grads_x[l, p] for p in range(N_PIPE)]) for l in range(2)])
    grad_w = jnp.stack([grads_w[p] for p in range(N_PIPE)])
    return (grad_x, grad_w)
```

```python
import functools

import jax
import jax.numpy as jnp
from jax import lax
from jax.experimental import pallas as pl
from jax.experimental.pallas import tpu as pltpu
from jax.sharding import PartitionSpec as P

HEAD = 128
BLOCKS = 2
CHUNKS = 8
EARLY = 6
MESH = pl.DeviceIdType.MESH
F32 = jnp.float32
BF16 = jnp.bfloat16


def kernel(
    npipe, ndp,
    x_ref, go_ref, g_ref, w_ref, gx_ref, gw_ref,
    wfull, ht, hall, dvall, vcur, vsend, cbuf, dhg, rinv,
    s1r, s0r, p1r, s1s, s0s, p1s,
    w_send, w_recv, f_send, f_recv, h_send, h_recv, d_send, d_recv,
    v_send, v_recv, s1_ss, s1_rs, s0_ss, s0_rs, p1_ss, p1_rs, loc,
):
    p = lax.axis_index("pipe")
    me = lax.axis_index("dp")
    tok, width = go_ref.shape
    kv = w_ref.shape[1]
    shard = w_ref.shape[0]
    group = width // kv
    tile = group * HEAD
    heads = kv // HEAD
    half = ndp // 2
    chip = me // 2
    core = me % 2
    sib = 2 * chip + 1 - core
    below = (p + npipe - 1) % npipe
    above = (p + 1) % npipe
    brow = tok // BLOCKS
    crow = tok // CHUNKS
    last = p == npipe - 1
    first = p == 0

    def remote(src, dst, ss, rs, pipe, dp):
        return pltpu.make_async_remote_copy(
            src_ref=src, dst_ref=dst, send_sem=ss, recv_sem=rs,
            device_id=(pipe, dp), device_id_type=MESH,
        )

    barrier = pltpu.get_barrier_semaphore()

    def greet(j, _):
        pl.semaphore_signal(
            barrier, inc=1, device_id=(p, (me + j) % ndp), device_id_type=MESH
        )
        return 0

    lax.fori_loop(1, ndp, greet, 0)
    pl.semaphore_signal(barrier, inc=1, device_id=(below, me), device_id_type=MESH)
    pl.semaphore_signal(barrier, inc=1, device_id=(above, me), device_id_type=MESH)
    pl.semaphore_wait(barrier, ndp + 1)

    def wrows(owner):
        return wfull.at[pl.ds(pl.multiple_of(owner * shard, shard), shard)]

    def w_copy(j):
        peer = 2 * ((chip + j) % half) + core
        return remote(w_ref, wrows(me), w_send.at[j], w_recv.at[j], p, peer)

    def f_copy(j):
        owner = 2 * ((chip + half - j) % half) + core
        return remote(wrows(owner), wrows(owner), f_send.at[j], f_recv.at[j], p, sib)

    f_own = remote(w_ref, wrows(me), f_send.at[0], f_recv.at[0], p, sib)

    def start_w(j, _):
        w_copy(j).start()
        return 0

    lax.fori_loop(1, half, start_w, 0)
    f_own.start()
    own_w = pltpu.make_async_copy(w_ref, wrows(me), loc.at[0])
    own_w.start()

    @pl.when(last)
    def _():
        s1r[...] = jnp.zeros_like(s1r)
        s0r[...] = jnp.zeros_like(s0r)
        for t in range(heads):
            acc = go_ref[:, t * tile:t * tile + HEAD].astype(F32)
            for r in range(1, group):
                lo = t * tile + r * HEAD
                acc = acc + go_ref[:, lo:lo + HEAD].astype(F32)
            vcur[1, :, t * HEAD:(t + 1) * HEAD] = acc.astype(BF16)

    @pl.when(first)
    def _():
        p1r[...] = jnp.zeros_like(p1r)

    for l in range(2):
        total = jnp.zeros((tok, HEAD), F32)
        for t in range(width // HEAD):
            xx = x_ref[l, :, t * HEAD:(t + 1) * HEAD].astype(F32)
            total = total + xx * xx
        mean = jnp.sum(total, axis=-1, keepdims=True) / width
        rinv[l] = jnp.broadcast_to(lax.rsqrt(mean + 1e-05), (tok, HEAD))
        for t in range(width // HEAD):
            cols = slice(t * HEAD, (t + 1) * HEAD)
            xn = x_ref[l, :, cols].astype(F32) * rinv[l]
            hid = xn * g_ref[l:l + 1, cols]
            ht[cols, l * tok:(l + 1) * tok] = hid.T.astype(BF16)

    def hrows(owner):
        return ht.at[pl.ds(pl.multiple_of(owner * shard, shard), shard)]

    wide = 2 * tok
    hslot = hall.at[:, pl.ds(pl.multiple_of(me * wide, wide), wide)]

    def h_copy(j):
        peer = (me + j) % ndp
        return remote(hrows(peer), hslot, h_send.at[j], h_recv.at[j], p, peer)

    def start_h(j, _):
        h_copy(j).start()
        return 0

    lax.fori_loop(1, ndp, start_h, 0)
    own_h = pltpu.make_async_copy(hrows(me), hslot, loc.at[1])
    own_h.start()

    def forward_w(j, _):
        w_copy(j).wait_recv()
        f_copy(j).start()
        return 0

    lax.fori_loop(1, half, forward_w, 0)
    own_w.wait()
    f_own.wait_recv()

    def arrived_w(j, _):
        f_copy(j).wait_recv()
        return 0

    lax.fori_loop(1, half, arrived_w, 0)

    def d_slot(l):
        return dvall.at[pl.ds(pl.multiple_of((me * 2 + l) * tok, tok), tok)]

    def d_copy(l, j):
        peer = (me + j) % ndp
        return remote(
            vcur.at[l], d_slot(l), d_send.at[l, j], d_recv.at[l, j], p, peer
        )

    def v_copy(l, b):
        slot = l - (npipe - 1 - p) // (npipe - 1)
        rows = pl.ds(b * brow, brow)
        return remote(
            vsend.at[l, rows], vcur.at[slot, rows],
            v_send.at[l, b], v_recv.at[slot, b], below, me,
        )

    def v_arrival(l, b):
        rows = pl.ds(b * brow, brow)
        return remote(
            vsend.at[l, rows], vcur.at[l, rows],
            v_send.at[l, b], v_recv.at[l, b], below, me,
        )

    def turn(l):
        for b in range(BLOCKS):
            rows = slice(b * brow, (b + 1) * brow)
            if l == 1:
                @pl.when(jnp.logical_not(last))
                def _():
                    v_arrival(l, b).wait_recv()
            else:
                v_arrival(l, b).wait_recv()
            vb = vcur[l, rows]
            ri = rinv[l, rows]
            total = jnp.zeros((brow, HEAD), F32)
            for t in range(heads):
                dh = lax.dot_general(
                    vb, wfull[t * tile:(t + 1) * tile],
                    (((1,), (1,)), ((), ())), preferred_element_type=F32,
                )
                for r in range(group):
                    cols = slice(t * tile + r * HEAD, t * tile + (r + 1) * HEAD)
                    d = dh[:, r * HEAD:(r + 1) * HEAD] * g_ref[l:l + 1, cols]
                    dhg[:, cols] = d
                    total = total + d * (x_ref[l, rows, cols].astype(F32) * ri)
            mean = jnp.sum(total, axis=-1, keepdims=True) / width
            for t in range(heads):
                acc = vb[:, t * HEAD:(t + 1) * HEAD].astype(F32)
                for r in range(group):
                    cols = slice(t * tile + r * HEAD, t * tile + (r + 1) * HEAD)
                    xn = x_ref[l, rows, cols].astype(F32) * ri
                    c = ri * (dhg[:, cols] - xn * mean)
                    cbuf[l, rows, cols] = c
                    acc = acc + c
                vsend[l, rows, t * HEAD:(t + 1) * HEAD] = acc.astype(BF16)
            if l == 1:
                v_copy(l, b).start()
            else:
                @pl.when(jnp.logical_not(first))
                def _():
                    v_copy(l, b).start()

        def start_d(j, _):
            d_copy(l, j).start()
            return 0

        lax.fori_loop(1, ndp, start_d, 0)
        own = pltpu.make_async_copy(vcur.at[l], d_slot(l), loc.at[2 + l])
        own.start()
        return own

    def crows(i):
        return pl.ds(pl.multiple_of(i * crow, crow), crow)

    def s1_copy(i):
        r = crows(i)
        return remote(s1s.at[r], s1r.at[r], s1_ss.at[i], s1_rs.at[i], below, me)

    def s0_copy(i):
        r = crows(i)
        return remote(s0s.at[r], s0r.at[r], s0_ss.at[i], s0_rs.at[i], below, me)

    def p1_copy(i):
        r = crows(i)
        return remote(p1s.at[r], p1r.at[r], p1_ss.at[i], p1_rs.at[i], above, me)

    def relay_s1(i, _):
        @pl.when(jnp.logical_not(last))
        def _():
            s1_copy(i).wait_recv()
        r = crows(i)
        s1 = cbuf[1, r] + s1r[r].astype(F32)
        s1s[r] = s1.astype(BF16)

        @pl.when(jnp.logical_not(first))
        def _():
            s1_copy(i).start()
        gx_ref[1, r] = (go_ref[r].astype(F32) + s1).astype(BF16)
        return 0

    def start_p1(i, _):
        r = crows(i)
        p1s[r] = cbuf[1, r].astype(BF16)
        p1_copy(i).start()
        return 0

    own_d1 = turn(1)

    @pl.when(first)
    def _():
        lax.fori_loop(0, CHUNKS, start_p1, 0)

    lax.fori_loop(0, EARLY, relay_s1, 0)

    @pl.when(last)
    def _():
        lax.fori_loop(EARLY, CHUNKS, relay_s1, 0)

    own_d0 = turn(0)

    @pl.when(jnp.logical_not(last))
    def _():
        lax.fori_loop(EARLY, CHUNKS, relay_s1, 0)

    def relay_rest(i, _):
        r = crows(i)

        @pl.when(jnp.logical_not(last))
        def _():
            s0_copy(i).wait_recv()
        s0 = cbuf[0, r] + s0r[r].astype(F32)

        @pl.when(jnp.logical_not(first))
        def _():
            s0s[r] = s0.astype(BF16)
            s0_copy(i).start()
        cbuf[0, r] = s0

        @pl.when(jnp.logical_not(first) & jnp.logical_not(last))
        def _():
            p1_copy(i).wait_recv()
            p1s[r] = (cbuf[1, r] + p1r[r].astype(F32)).astype(BF16)
            p1_copy(i).start()
        return 0

    def finish(i, _):
        r = crows(i)

        @pl.when(last)
        def _():
            p1_copy(i).wait_recv()
        dy = go_ref[r].astype(F32) + (cbuf[1, r] + s1r[r].astype(F32))
        gx_ref[0, r] = (dy + p1r[r].astype(F32) + cbuf[0, r]).astype(BF16)
        return 0

    lax.fori_loop(0, CHUNKS, relay_rest, 0)

    def arrived_h(j, _):
        h_copy(j).wait_recv()
        d_copy(0, j).wait_recv()
        d_copy(1, j).wait_recv()
        return 0

    lax.fori_loop(1, ndp, arrived_h, 0)
    own_h.wait()
    own_d1.wait()
    own_d0.wait()
    depth = ndp * wide
    step = min(depth, 2048)

    def product(k):
        cols = pl.ds(pl.multiple_of(k * step, step), step)
        return jnp.dot(hall[:, cols], dvall[cols], preferred_element_type=F32)

    gw_ref[...] = product(0)

    def more(k, _):
        gw_ref[...] += product(k)
        return 0

    if depth > step:
        lax.fori_loop(1, depth // step, more, 0)

    lax.fori_loop(0, CHUNKS, finish, 0)

    def sent_w(j, _):
        w_copy(j).wait_send()
        f_copy(j).wait_send()
        return 0

    lax.fori_loop(1, half, sent_w, 0)
    f_own.wait_send()

    def sent_h(j, _):
        h_copy(j).wait_send()
        d_copy(0, j).wait_send()
        d_copy(1, j).wait_send()
        return 0

    lax.fori_loop(1, ndp, sent_h, 0)
    for b in range(BLOCKS):
        v_copy(1, b).wait_send()

    def sent_s(i, _):
        s1_copy(i).wait_send()
        s0_copy(i).wait_send()
        return 0

    def sent_p(i, _):
        p1_copy(i).wait_send()
        return 0

    @pl.when(jnp.logical_not(first))
    def _():
        for b in range(BLOCKS):
            v_copy(0, b).wait_send()
        lax.fori_loop(0, CHUNKS, sent_s, 0)

    @pl.when(jnp.logical_not(last))
    def _():
        lax.fori_loop(0, CHUNKS, sent_p, 0)


def on_device(saved, grad_out, gain, w_value):
    npipe = lax.axis_size("pipe")
    ndp = lax.axis_size("dp")
    tok, width = grad_out.shape
    shard, kv = w_value.shape[1:]
    wide = 2 * tok
    dma = pltpu.SemaphoreType.DMA
    vmem = pl.BlockSpec(memory_space=pltpu.VMEM)
    gx, gw = pl.pallas_call(
        functools.partial(kernel, npipe, ndp),
        out_shape=(
            jax.ShapeDtypeStruct((2, tok, width), BF16),
            jax.ShapeDtypeStruct((shard, kv), F32),
        ),
        in_specs=[vmem] * 4,
        out_specs=(vmem, vmem),
        scratch_shapes=[
            pltpu.VMEM((width, kv), BF16),
            pltpu.VMEM((width, wide), BF16),
            pltpu.VMEM((shard, ndp * wide), BF16),
            pltpu.VMEM((ndp * wide, kv), BF16),
            pltpu.VMEM((2, tok, kv), BF16),
            pltpu.VMEM((2, tok, kv), BF16),
            pltpu.VMEM((2, tok, width), F32),
            pltpu.VMEM((tok // BLOCKS, width), F32),
            pltpu.VMEM((2, tok, HEAD), F32),
        ]
        + [pltpu.VMEM((tok, width), BF16)] * 6
        + [dma((ndp,))] * 6
        + [dma((2, ndp))] * 2
        + [dma((2, BLOCKS))] * 2
        + [dma((CHUNKS,))] * 6
        + [dma((4,))],
        compiler_params=pltpu.CompilerParams(
            collective_id=0, has_side_effects=True, vmem_limit_bytes=60 * 1024 * 1024
        ),
    )(saved[:, 0], grad_out, gain[:, 0], w_value[0])
    return gx[:, None], gw[None]


def solution(mesh):
    return jax.shard_map(
        on_device,
        mesh=mesh,
        in_specs=(
            P(None, "pipe", "dp", None),
            P("dp", None),
            P(None, "pipe", None),
            P("pipe", "dp", None),
        ),
        out_specs=(P(None, "pipe", "dp", None), P("pipe", "dp", None)),
        check_vma=False,
    )
```

```python
import functools

import jax
import jax.numpy as jnp
from jax import lax
from jax.experimental import pallas as pl
from jax.experimental.pallas import tpu as pltpu
from jax.sharding import PartitionSpec as P

HEAD = 128
BLOCKS = 2
CHUNKS = 8
EARLY = 6
AHEAD = 3
MESH = pl.DeviceIdType.MESH
F32 = jnp.float32
BF16 = jnp.bfloat16


def kernel(
    npipe, ndp,
    x_ref, go_ref, g_ref, w_ref, gx_ref, gw_ref,
    wfull, ht, hall, dvall, vcur, vsend, cbuf, dhg, rinv,
    s1r, s0r, p1r, s1s, s0s, p1s,
    w_send, w_recv, f_send, f_recv, h_send, h_recv, d_send, d_recv,
    v_send, v_recv, s1_ss, s1_rs, s0_ss, s0_rs, p1_ss, p1_rs, loc,
):
    p = lax.axis_index("pipe")
    me = lax.axis_index("dp")
    tok, width = go_ref.shape
    kv = w_ref.shape[1]
    shard = w_ref.shape[0]
    group = width // kv
    tile = group * HEAD
    heads = kv // HEAD
    half = ndp // 2
    chip = me // 2
    core = me % 2
    sib = 2 * chip + 1 - core
    below = (p + npipe - 1) % npipe
    above = (p + 1) % npipe
    brow = tok // BLOCKS
    crow = tok // CHUNKS
    last = p == npipe - 1
    first = p == 0

    def remote(src, dst, ss, rs, pipe, dp):
        return pltpu.make_async_remote_copy(
            src_ref=src, dst_ref=dst, send_sem=ss, recv_sem=rs,
            device_id=(pipe, dp), device_id_type=MESH,
        )

    barrier = pltpu.get_barrier_semaphore()

    def greet(j, _):
        pl.semaphore_signal(
            barrier, inc=1, device_id=(p, (me + j) % ndp), device_id_type=MESH
        )
        return 0

    lax.fori_loop(1, ndp, greet, 0)
    pl.semaphore_signal(barrier, inc=1, device_id=(below, me), device_id_type=MESH)
    pl.semaphore_signal(barrier, inc=1, device_id=(above, me), device_id_type=MESH)
    pl.semaphore_wait(barrier, ndp + 1)

    def wrows(owner):
        return wfull.at[pl.ds(pl.multiple_of(owner * shard, shard), shard)]

    def w_copy(j):
        peer = 2 * ((chip + j) % half) + core
        return remote(w_ref, wrows(me), w_send.at[j], w_recv.at[j], p, peer)

    def f_copy(j):
        owner = 2 * ((chip + half - j) % half) + core
        return remote(wrows(owner), wrows(owner), f_send.at[j], f_recv.at[j], p, sib)

    f_own = remote(w_ref, wrows(me), f_send.at[0], f_recv.at[0], p, sib)

    def start_w(j, _):
        w_copy(j).start()
        return 0

    lax.fori_loop(1, half, start_w, 0)
    f_own.start()
    own_w = pltpu.make_async_copy(w_ref, wrows(me), loc.at[0])
    own_w.start()

    @pl.when(last)
    def _():
        s1r[...] = jnp.zeros_like(s1r)
        s0r[...] = jnp.zeros_like(s0r)
        for t in range(heads):
            acc = go_ref[:, t * tile:t * tile + HEAD].astype(F32)
            for r in range(1, group):
                lo = t * tile + r * HEAD
                acc = acc + go_ref[:, lo:lo + HEAD].astype(F32)
            vcur[1, :, t * HEAD:(t + 1) * HEAD] = acc.astype(BF16)

    @pl.when(first)
    def _():
        p1r[...] = jnp.zeros_like(p1r)

    for l in range(2):
        total = jnp.zeros((tok, HEAD), F32)
        for t in range(width // HEAD):
            xx = x_ref[l, :, t * HEAD:(t + 1) * HEAD].astype(F32)
            total = total + xx * xx
        mean = jnp.sum(total, axis=-1, keepdims=True) / width
        rinv[l] = jnp.broadcast_to(lax.rsqrt(mean + 1e-05), (tok, HEAD))
        for t in range(width // HEAD):
            cols = slice(t * HEAD, (t + 1) * HEAD)
            xn = x_ref[l, :, cols].astype(F32) * rinv[l]
            hid = xn * g_ref[l:l + 1, cols]
            ht[cols, l * tok:(l + 1) * tok] = hid.T.astype(BF16)

    def hrows(owner):
        return ht.at[pl.ds(pl.multiple_of(owner * shard, shard), shard)]

    wide = 2 * tok
    hslot = hall.at[:, pl.ds(pl.multiple_of(me * wide, wide), wide)]

    def h_copy(j):
        peer = (me + j) % ndp
        return remote(hrows(peer), hslot, h_send.at[j], h_recv.at[j], p, peer)

    def start_h(j, _):
        h_copy(j).start()
        return 0

    lax.fori_loop(1, ndp, start_h, 0)
    own_h = pltpu.make_async_copy(hrows(me), hslot, loc.at[1])
    own_h.start()

    def forward_w(j, _):
        w_copy(j).wait_recv()
        f_copy(j).start()
        return 0

    lax.fori_loop(1, half, forward_w, 0)
    own_w.wait()
    f_own.wait_recv()

    def arrived_w(j, _):
        f_copy(j).wait_recv()
        return 0

    lax.fori_loop(1, half, arrived_w, 0)

    def d_slot(l):
        return dvall.at[pl.ds(pl.multiple_of((me * 2 + l) * tok, tok), tok)]

    def d_copy(l, j):
        peer = (me + j) % ndp
        return remote(
            vcur.at[l], d_slot(l), d_send.at[l, j], d_recv.at[l, j], p, peer
        )

    def v_copy(l, b):
        slot = l - (npipe - 1 - p) // (npipe - 1)
        rows = pl.ds(b * brow, brow)
        return remote(
            vsend.at[l, rows], vcur.at[slot, rows],
            v_send.at[l, b], v_recv.at[slot, b], below, me,
        )

    def v_arrival(l, b):
        rows = pl.ds(b * brow, brow)
        return remote(
            vsend.at[l, rows], vcur.at[l, rows],
            v_send.at[l, b], v_recv.at[l, b], below, me,
        )

    def turn(l):
        for b in range(BLOCKS):
            rows = slice(b * brow, (b + 1) * brow)
            if l == 1:
                @pl.when(jnp.logical_not(last))
                def _():
                    v_arrival(l, b).wait_recv()
            else:
                v_arrival(l, b).wait_recv()
            vb = vcur[l, rows]
            ri = rinv[l, rows]
            total = jnp.zeros((brow, HEAD), F32)
            for t in range(heads):
                dh = lax.dot_general(
                    vb, wfull[t * tile:(t + 1) * tile],
                    (((1,), (1,)), ((), ())), preferred_element_type=F32,
                )
                for r in range(group):
                    cols = slice(t * tile + r * HEAD, t * tile + (r + 1) * HEAD)
                    d = dh[:, r * HEAD:(r + 1) * HEAD] * g_ref[l:l + 1, cols]
                    dhg[:, cols] = d
                    total = total + d * (x_ref[l, rows, cols].astype(F32) * ri)
            mean = jnp.sum(total, axis=-1, keepdims=True) / width
            for t in range(heads):
                acc = vb[:, t * HEAD:(t + 1) * HEAD].astype(F32)
                for r in range(group):
                    cols = slice(t * tile + r * HEAD, t * tile + (r + 1) * HEAD)
                    xn = x_ref[l, rows, cols].astype(F32) * ri
                    c = ri * (dhg[:, cols] - xn * mean)
                    cbuf[l, rows, cols] = c
                    acc = acc + c
                vsend[l, rows, t * HEAD:(t + 1) * HEAD] = acc.astype(BF16)
            if l == 1:
                v_copy(l, b).start()
            else:
                @pl.when(jnp.logical_not(first))
                def _():
                    v_copy(l, b).start()

        def start_d(j, _):
            d_copy(l, j).start()
            return 0

        lax.fori_loop(1, ndp, start_d, 0)
        own = pltpu.make_async_copy(vcur.at[l], d_slot(l), loc.at[2 + l])
        own.start()
        return own

    def crows(i):
        return pl.ds(pl.multiple_of(i * crow, crow), crow)

    def s1_copy(i):
        r = crows(i)
        return remote(s1s.at[r], s1r.at[r], s1_ss.at[i], s1_rs.at[i], below, me)

    def s0_copy(i):
        r = crows(i)
        return remote(s0s.at[r], s0r.at[r], s0_ss.at[i], s0_rs.at[i], below, me)

    def p1_copy(i):
        r = crows(i)
        return remote(p1s.at[r], p1r.at[r], p1_ss.at[i], p1_rs.at[i], above, me)

    def relay_s1(i, _):
        @pl.when(jnp.logical_not(last))
        def _():
            s1_copy(i).wait_recv()
        r = crows(i)
        s1 = cbuf[1, r] + s1r[r].astype(F32)
        s1s[r] = s1.astype(BF16)

        @pl.when(jnp.logical_not(first))
        def _():
            s1_copy(i).start()
        gx_ref[1, r] = (go_ref[r].astype(F32) + s1).astype(BF16)
        return 0

    def start_p1(i, _):
        r = crows(i)
        p1s[r] = cbuf[1, r].astype(BF16)
        p1_copy(i).start()
        return 0

    own_d1 = turn(1)

    @pl.when(first)
    def _():
        lax.fori_loop(0, CHUNKS, start_p1, 0)

    lax.fori_loop(0, EARLY, relay_s1, 0)

    @pl.when(last)
    def _():
        lax.fori_loop(EARLY, CHUNKS, relay_s1, 0)

    own_d0 = turn(0)

    @pl.when(jnp.logical_not(last))
    def _():
        lax.fori_loop(EARLY, CHUNKS, relay_s1, 0)

    def relay_s0(i, _):
        r = crows(i)

        @pl.when(jnp.logical_not(last))
        def _():
            s0_copy(i).wait_recv()
        s0 = cbuf[0, r] + s0r[r].astype(F32)

        @pl.when(jnp.logical_not(first))
        def _():
            s0s[r] = s0.astype(BF16)
            s0_copy(i).start()
        cbuf[0, r] = s0
        return 0

    def relay_p1(i, _):
        r = crows(i)

        @pl.when(jnp.logical_not(first) & jnp.logical_not(last))
        def _():
            p1_copy(i).wait_recv()
            p1s[r] = (cbuf[1, r] + p1r[r].astype(F32)).astype(BF16)
            p1_copy(i).start()
        return 0

    def relay_both(i, _):
        relay_p1(i + AHEAD, 0)
        return relay_s0(i, 0)

    def finish(i, _):
        r = crows(i)

        @pl.when(last)
        def _():
            p1_copy(i).wait_recv()
        dy = go_ref[r].astype(F32) + (cbuf[1, r] + s1r[r].astype(F32))
        gx_ref[0, r] = (dy + p1r[r].astype(F32) + cbuf[0, r]).astype(BF16)
        return 0

    lax.fori_loop(0, AHEAD, relay_p1, 0)
    lax.fori_loop(0, CHUNKS - AHEAD, relay_both, 0)
    lax.fori_loop(CHUNKS - AHEAD, CHUNKS, relay_s0, 0)

    def arrived_h(j, _):
        h_copy(j).wait_recv()
        d_copy(0, j).wait_recv()
        d_copy(1, j).wait_recv()
        return 0

    lax.fori_loop(1, ndp, arrived_h, 0)
    own_h.wait()
    own_d1.wait()
    own_d0.wait()
    depth = ndp * wide
    step = min(depth, 2048)

    def product(k):
        cols = pl.ds(pl.multiple_of(k * step, step), step)
        return jnp.dot(hall[:, cols], dvall[cols], preferred_element_type=F32)

    gw_ref[...] = product(0)

    def more(k, _):
        gw_ref[...] += product(k)
        return 0

    if depth > step:
        lax.fori_loop(1, depth // step, more, 0)

    lax.fori_loop(0, CHUNKS, finish, 0)

    def sent_w(j, _):
        w_copy(j).wait_send()
        f_copy(j).wait_send()
        return 0

    lax.fori_loop(1, half, sent_w, 0)
    f_own.wait_send()

    def sent_h(j, _):
        h_copy(j).wait_send()
        d_copy(0, j).wait_send()
        d_copy(1, j).wait_send()
        return 0

    lax.fori_loop(1, ndp, sent_h, 0)
    for b in range(BLOCKS):
        v_copy(1, b).wait_send()

    def sent_s(i, _):
        s1_copy(i).wait_send()
        s0_copy(i).wait_send()
        return 0

    def sent_p(i, _):
        p1_copy(i).wait_send()
        return 0

    @pl.when(jnp.logical_not(first))
    def _():
        for b in range(BLOCKS):
            v_copy(0, b).wait_send()
        lax.fori_loop(0, CHUNKS, sent_s, 0)

    @pl.when(jnp.logical_not(last))
    def _():
        lax.fori_loop(0, CHUNKS, sent_p, 0)


def on_device(saved, grad_out, gain, w_value):
    npipe = lax.axis_size("pipe")
    ndp = lax.axis_size("dp")
    tok, width = grad_out.shape
    shard, kv = w_value.shape[1:]
    wide = 2 * tok
    dma = pltpu.SemaphoreType.DMA
    vmem = pl.BlockSpec(memory_space=pltpu.VMEM)
    gx, gw = pl.pallas_call(
        functools.partial(kernel, npipe, ndp),
        out_shape=(
            jax.ShapeDtypeStruct((2, tok, width), BF16),
            jax.ShapeDtypeStruct((shard, kv), F32),
        ),
        in_specs=[vmem] * 4,
        out_specs=(vmem, vmem),
        scratch_shapes=[
            pltpu.VMEM((width, kv), BF16),
            pltpu.VMEM((width, wide), BF16),
            pltpu.VMEM((shard, ndp * wide), BF16),
            pltpu.VMEM((ndp * wide, kv), BF16),
            pltpu.VMEM((2, tok, kv), BF16),
            pltpu.VMEM((2, tok, kv), BF16),
            pltpu.VMEM((2, tok, width), F32),
            pltpu.VMEM((tok // BLOCKS, width), F32),
            pltpu.VMEM((2, tok, HEAD), F32),
        ]
        + [pltpu.VMEM((tok, width), BF16)] * 6
        + [dma((ndp,))] * 6
        + [dma((2, ndp))] * 2
        + [dma((2, BLOCKS))] * 2
        + [dma((CHUNKS,))] * 6
        + [dma((4,))],
        compiler_params=pltpu.CompilerParams(
            collective_id=0, has_side_effects=True, vmem_limit_bytes=60 * 1024 * 1024
        ),
    )(saved[:, 0], grad_out, gain[:, 0], w_value[0])
    return gx[:, None], gw[None]


def solution(mesh):
    return jax.shard_map(
        on_device,
        mesh=mesh,
        in_specs=(
            P(None, "pipe", "dp", None),
            P("dp", None),
            P(None, "pipe", None),
            P("pipe", "dp", None),
        ),
        out_specs=(P(None, "pipe", "dp", None), P("pipe", "dp", None)),
        check_vma=False,
    )
```

```python
import functools

import jax
import jax.numpy as jnp
from jax import lax
from jax.experimental import pallas as pl
from jax.experimental.pallas import tpu as pltpu
from jax.sharding import PartitionSpec as P

HEAD = 128
BLOCKS = 2
CHUNKS = 8
EARLY = 5
WINDOW = 2
AHEAD = 3
MESH = pl.DeviceIdType.MESH
F32 = jnp.float32
BF16 = jnp.bfloat16


def kernel(
    npipe, ndp,
    x_ref, go_ref, g_ref, w_ref, gx_ref, gw_ref,
    wfull, ht, hall, dvall, vcur, vsend, cbuf, dhg, rinv,
    s1r, s0r, p1r, s1s, s0s, p1s,
    w_send, w_recv, f_send, f_recv, h_send, h_recv, d_send, d_recv,
    v_send, v_recv, s1_ss, s1_rs, s0_ss, s0_rs, p1_ss, p1_rs, loc,
):
    p = lax.axis_index("pipe")
    me = lax.axis_index("dp")
    tok, width = go_ref.shape
    kv = w_ref.shape[1]
    shard = w_ref.shape[0]
    group = width // kv
    tile = group * HEAD
    heads = kv // HEAD
    half = ndp // 2
    chip = me // 2
    core = me % 2
    sib = 2 * chip + 1 - core
    below = (p + npipe - 1) % npipe
    above = (p + 1) % npipe
    brow = tok // BLOCKS
    crow = tok // CHUNKS
    last = p == npipe - 1
    first = p == 0

    def remote(src, dst, ss, rs, pipe, dp):
        return pltpu.make_async_remote_copy(
            src_ref=src, dst_ref=dst, send_sem=ss, recv_sem=rs,
            device_id=(pipe, dp), device_id_type=MESH,
        )

    barrier = pltpu.get_barrier_semaphore()

    def greet(j, _):
        pl.semaphore_signal(
            barrier, inc=1, device_id=(p, (me + j) % ndp), device_id_type=MESH
        )
        return 0

    lax.fori_loop(1, ndp, greet, 0)
    pl.semaphore_signal(barrier, inc=1, device_id=(below, me), device_id_type=MESH)
    pl.semaphore_signal(barrier, inc=1, device_id=(above, me), device_id_type=MESH)
    pl.semaphore_wait(barrier, ndp + 1)

    def wrows(owner):
        return wfull.at[pl.ds(pl.multiple_of(owner * shard, shard), shard)]

    def w_copy(j):
        peer = 2 * ((chip + j) % half) + core
        return remote(w_ref, wrows(me), w_send.at[j], w_recv.at[j], p, peer)

    def f_copy(j):
        owner = 2 * ((chip + half - j) % half) + core
        return remote(wrows(owner), wrows(owner), f_send.at[j], f_recv.at[j], p, sib)

    f_own = remote(w_ref, wrows(me), f_send.at[0], f_recv.at[0], p, sib)

    def start_w(j, _):
        w_copy(j).start()
        return 0

    lax.fori_loop(1, half, start_w, 0)
    f_own.start()
    own_w = pltpu.make_async_copy(w_ref, wrows(me), loc.at[0])
    own_w.start()

    @pl.when(last)
    def _():
        s1r[...] = jnp.zeros_like(s1r)
        s0r[...] = jnp.zeros_like(s0r)
        for t in range(heads):
            acc = go_ref[:, t * tile:t * tile + HEAD].astype(F32)
            for r in range(1, group):
                lo = t * tile + r * HEAD
                acc = acc + go_ref[:, lo:lo + HEAD].astype(F32)
            vcur[1, :, t * HEAD:(t + 1) * HEAD] = acc.astype(BF16)

    @pl.when(first)
    def _():
        p1r[...] = jnp.zeros_like(p1r)

    for l in range(2):
        total = jnp.zeros((tok, HEAD), F32)
        for t in range(width // HEAD):
            xx = x_ref[l, :, t * HEAD:(t + 1) * HEAD].astype(F32)
            total = total + xx * xx
        mean = jnp.sum(total, axis=-1, keepdims=True) / width
        rinv[l] = jnp.broadcast_to(lax.rsqrt(mean + 1e-05), (tok, HEAD))
        for t in range(width // HEAD):
            cols = slice(t * HEAD, (t + 1) * HEAD)
            xn = x_ref[l, :, cols].astype(F32) * rinv[l]
            hid = xn * g_ref[l:l + 1, cols]
            ht[cols, l * tok:(l + 1) * tok] = hid.T.astype(BF16)

    def hrows(owner):
        return ht.at[pl.ds(pl.multiple_of(owner * shard, shard), shard)]

    wide = 2 * tok
    hslot = hall.at[:, pl.ds(pl.multiple_of(me * wide, wide), wide)]

    def h_copy(j):
        peer = (me + j) % ndp
        return remote(hrows(peer), hslot, h_send.at[j], h_recv.at[j], p, peer)

    def start_h(j, _):
        h_copy(j).start()
        return 0

    lax.fori_loop(1, ndp, start_h, 0)
    own_h = pltpu.make_async_copy(hrows(me), hslot, loc.at[1])
    own_h.start()

    def forward_w(j, _):
        w_copy(j).wait_recv()
        f_copy(j).start()
        return 0

    lax.fori_loop(1, half, forward_w, 0)
    own_w.wait()
    f_own.wait_recv()

    def arrived_w(j, _):
        f_copy(j).wait_recv()
        return 0

    lax.fori_loop(1, half, arrived_w, 0)

    def d_slot(l):
        return dvall.at[pl.ds(pl.multiple_of((me * 2 + l) * tok, tok), tok)]

    def d_copy(l, j):
        peer = (me + j) % ndp
        return remote(
            vcur.at[l], d_slot(l), d_send.at[l, j], d_recv.at[l, j], p, peer
        )

    def v_copy(l, b):
        slot = l - (npipe - 1 - p) // (npipe - 1)
        rows = pl.ds(b * brow, brow)
        return remote(
            vsend.at[l, rows], vcur.at[slot, rows],
            v_send.at[l, b], v_recv.at[slot, b], below, me,
        )

    def v_arrival(l, b):
        rows = pl.ds(b * brow, brow)
        return remote(
            vsend.at[l, rows], vcur.at[l, rows],
            v_send.at[l, b], v_recv.at[l, b], below, me,
        )

    def turn(l):
        for b in range(BLOCKS):
            rows = slice(b * brow, (b + 1) * brow)
            if l == 1:
                @pl.when(jnp.logical_not(last))
                def _():
                    v_arrival(l, b).wait_recv()
            else:
                v_arrival(l, b).wait_recv()
            vb = vcur[l, rows]
            ri = rinv[l, rows]
            total = jnp.zeros((brow, HEAD), F32)
            for t in range(heads):
                dh = lax.dot_general(
                    vb, wfull[t * tile:(t + 1) * tile],
                    (((1,), (1,)), ((), ())), preferred_element_type=F32,
                )
                for r in range(group):
                    cols = slice(t * tile + r * HEAD, t * tile + (r + 1) * HEAD)
                    d = dh[:, r * HEAD:(r + 1) * HEAD] * g_ref[l:l + 1, cols]
                    dhg[:, cols] = d
                    total = total + d * (x_ref[l, rows, cols].astype(F32) * ri)
            mean = jnp.sum(total, axis=-1, keepdims=True) / width
            for t in range(heads):
                acc = vb[:, t * HEAD:(t + 1) * HEAD].astype(F32)
                for r in range(group):
                    cols = slice(t * tile + r * HEAD, t * tile + (r + 1) * HEAD)
                    xn = x_ref[l, rows, cols].astype(F32) * ri
                    c = ri * (dhg[:, cols] - xn * mean)
                    cbuf[l, rows, cols] = c
                    acc = acc + c
                vsend[l, rows, t * HEAD:(t + 1) * HEAD] = acc.astype(BF16)
            if l == 1:
                v_copy(l, b).start()
            else:
                @pl.when(jnp.logical_not(first))
                def _():
                    v_copy(l, b).start()

        def start_d(j, _):
            d_copy(l, j).start()
            return 0

        lax.fori_loop(1, ndp, start_d, 0)
        own = pltpu.make_async_copy(vcur.at[l], d_slot(l), loc.at[2 + l])
        own.start()
        return own

    def crows(i):
        return pl.ds(pl.multiple_of(i * crow, crow), crow)

    def s1_copy(i):
        r = crows(i)
        return remote(s1s.at[r], s1r.at[r], s1_ss.at[i], s1_rs.at[i], below, me)

    def s0_copy(i):
        r = crows(i)
        return remote(s0s.at[r], s0r.at[r], s0_ss.at[i], s0_rs.at[i], below, me)

    def p1_copy(i):
        r = crows(i)
        return remote(p1s.at[r], p1r.at[r], p1_ss.at[i], p1_rs.at[i], above, me)

    def windowed(copy, i):
        @pl.when(i >= WINDOW)
        def _():
            copy(i - WINDOW).wait_send()
        copy(i).start()

    def relay_s1(i, _):
        @pl.when(jnp.logical_not(last))
        def _():
            s1_copy(i).wait_recv()
        r = crows(i)
        s1 = cbuf[1, r] + s1r[r].astype(F32)
        s1s[r] = s1.astype(BF16)

        @pl.when(jnp.logical_not(first))
        def _():
            windowed(s1_copy, i)

        @pl.when(first)
        def _():
            p1s[r] = cbuf[1, r].astype(BF16)
            windowed(p1_copy, i)
        gx_ref[1, r] = (go_ref[r].astype(F32) + s1).astype(BF16)
        return 0

    own_d1 = turn(1)

    lax.fori_loop(0, EARLY, relay_s1, 0)
    own_d0 = turn(0)
    lax.fori_loop(EARLY, CHUNKS, relay_s1, 0)

    def relay_s0(i, _):
        r = crows(i)

        @pl.when(jnp.logical_not(last))
        def _():
            s0_copy(i).wait_recv()
        s0 = cbuf[0, r] + s0r[r].astype(F32)

        @pl.when(jnp.logical_not(first))
        def _():
            s0s[r] = s0.astype(BF16)
            windowed(s0_copy, i)
        cbuf[0, r] = s0
        return 0

    def relay_p1(i, _):
        r = crows(i)

        @pl.when(jnp.logical_not(first) & jnp.logical_not(last))
        def _():
            p1_copy(i).wait_recv()
            p1s[r] = (cbuf[1, r] + p1r[r].astype(F32)).astype(BF16)
            windowed(p1_copy, i)
        return 0

    def relay_both(i, _):
        relay_p1(i + AHEAD, 0)
        return relay_s0(i, 0)

    def finish(i, _):
        r = crows(i)

        @pl.when(last)
        def _():
            p1_copy(i).wait_recv()
        dy = go_ref[r].astype(F32) + (cbuf[1, r] + s1r[r].astype(F32))
        gx_ref[0, r] = (dy + p1r[r].astype(F32) + cbuf[0, r]).astype(BF16)
        return 0

    lax.fori_loop(0, AHEAD, relay_p1, 0)
    lax.fori_loop(0, CHUNKS - AHEAD, relay_both, 0)
    lax.fori_loop(CHUNKS - AHEAD, CHUNKS, relay_s0, 0)

    def arrived_h(j, _):
        h_copy(j).wait_recv()
        d_copy(0, j).wait_recv()
        d_copy(1, j).wait_recv()
        return 0

    lax.fori_loop(1, ndp, arrived_h, 0)
    own_h.wait()
    own_d1.wait()
    own_d0.wait()
    depth = ndp * wide
    step = min(depth, 2048)

    def product(k):
        cols = pl.ds(pl.multiple_of(k * step, step), step)
        return jnp.dot(hall[:, cols], dvall[cols], preferred_element_type=F32)

    gw_ref[...] = product(0)

    def more(k, _):
        gw_ref[...] += product(k)
        return 0

    if depth > step:
        lax.fori_loop(1, depth // step, more, 0)

    lax.fori_loop(0, CHUNKS, finish, 0)

    def sent_w(j, _):
        w_copy(j).wait_send()
        f_copy(j).wait_send()
        return 0

    lax.fori_loop(1, half, sent_w, 0)
    f_own.wait_send()

    def sent_h(j, _):
        h_copy(j).wait_send()
        d_copy(0, j).wait_send()
        d_copy(1, j).wait_send()
        return 0

    lax.fori_loop(1, ndp, sent_h, 0)
    for b in range(BLOCKS):
        v_copy(1, b).wait_send()

    def sent_s(i, _):
        s1_copy(i).wait_send()
        s0_copy(i).wait_send()
        return 0

    def sent_p(i, _):
        p1_copy(i).wait_send()
        return 0

    @pl.when(jnp.logical_not(first))
    def _():
        for b in range(BLOCKS):
            v_copy(0, b).wait_send()
        lax.fori_loop(CHUNKS - WINDOW, CHUNKS, sent_s, 0)

    @pl.when(jnp.logical_not(last))
    def _():
        lax.fori_loop(CHUNKS - WINDOW, CHUNKS, sent_p, 0)


def on_device(saved, grad_out, gain, w_value):
    npipe = lax.axis_size("pipe")
    ndp = lax.axis_size("dp")
    tok, width = grad_out.shape
    shard, kv = w_value.shape[1:]
    wide = 2 * tok
    dma = pltpu.SemaphoreType.DMA
    vmem = pl.BlockSpec(memory_space=pltpu.VMEM)
    gx, gw = pl.pallas_call(
        functools.partial(kernel, npipe, ndp),
        out_shape=(
            jax.ShapeDtypeStruct((2, tok, width), BF16),
            jax.ShapeDtypeStruct((shard, kv), F32),
        ),
        in_specs=[vmem] * 4,
        out_specs=(vmem, vmem),
        scratch_shapes=[
            pltpu.VMEM((width, kv), BF16),
            pltpu.VMEM((width, wide), BF16),
            pltpu.VMEM((shard, ndp * wide), BF16),
            pltpu.VMEM((ndp * wide, kv), BF16),
            pltpu.VMEM((2, tok, kv), BF16),
            pltpu.VMEM((2, tok, kv), BF16),
            pltpu.VMEM((2, tok, width), F32),
            pltpu.VMEM((tok // BLOCKS, width), F32),
            pltpu.VMEM((2, tok, HEAD), F32),
        ]
        + [pltpu.VMEM((tok, width), BF16)] * 6
        + [dma((ndp,))] * 6
        + [dma((2, ndp))] * 2
        + [dma((2, BLOCKS))] * 2
        + [dma((CHUNKS,))] * 6
        + [dma((4,))],
        compiler_params=pltpu.CompilerParams(
            collective_id=0, has_side_effects=True, vmem_limit_bytes=60 * 1024 * 1024
        ),
    )(saved[:, 0], grad_out, gain[:, 0], w_value[0])
    return gx[:, None], gw[None]


def solution(mesh):
    return jax.shard_map(
        on_device,
        mesh=mesh,
        in_specs=(
            P(None, "pipe", "dp", None),
            P("dp", None),
            P(None, "pipe", None),
            P("pipe", "dp", None),
        ),
        out_specs=(P(None, "pipe", "dp", None), P("pipe", "dp", None)),
        check_vma=False,
    )
```

```python
import functools

import jax
import jax.numpy as jnp
from jax import lax
from jax.experimental import pallas as pl
from jax.experimental.pallas import tpu as pltpu
from jax.sharding import PartitionSpec as P

HEAD = 128
BLOCKS = 2
CHUNKS = 8
EARLY = 5
WINDOW = 2
AHEAD = 3
MESH = pl.DeviceIdType.MESH
F32 = jnp.float32
BF16 = jnp.bfloat16


def kernel(
    npipe, ndp,
    x_ref, go_ref, g_ref, w_ref, gx_ref, gw_ref,
    wfull, ht, hall, dvall, vcur, vsend, cbuf, dhg, rinv,
    s1r, s0r, p1r, s1s, s0s, p1s,
    w_send, w_recv, f_send, f_recv, h_send, h_recv, d_send, d_recv,
    v_send, v_recv, s1_ss, s1_rs, s0_ss, s0_rs, p1_ss, p1_rs, loc,
):
    p = lax.axis_index("pipe")
    me = lax.axis_index("dp")
    tok, width = go_ref.shape
    kv = w_ref.shape[1]
    shard = w_ref.shape[0]
    group = width // kv
    tile = group * HEAD
    heads = kv // HEAD
    half = ndp // 2
    chip = me // 2
    core = me % 2
    sib = 2 * chip + 1 - core
    below = (p + npipe - 1) % npipe
    above = (p + 1) % npipe
    brow = tok // BLOCKS
    crow = tok // CHUNKS
    last = p == npipe - 1
    first = p == 0

    def remote(src, dst, ss, rs, pipe, dp):
        return pltpu.make_async_remote_copy(
            src_ref=src, dst_ref=dst, send_sem=ss, recv_sem=rs,
            device_id=(pipe, dp), device_id_type=MESH,
        )

    barrier = pltpu.get_barrier_semaphore()

    def greet(j, _):
        pl.semaphore_signal(
            barrier, inc=1, device_id=(p, (me + j) % ndp), device_id_type=MESH
        )
        return 0

    lax.fori_loop(1, ndp, greet, 0)
    pl.semaphore_signal(barrier, inc=1, device_id=(below, me), device_id_type=MESH)
    pl.semaphore_signal(barrier, inc=1, device_id=(above, me), device_id_type=MESH)
    pl.semaphore_wait(barrier, ndp + 1)

    def wrows(owner):
        return wfull.at[pl.ds(pl.multiple_of(owner * shard, shard), shard)]

    def w_copy(j):
        peer = 2 * ((chip + j) % half) + core
        return remote(w_ref, wrows(me), w_send.at[j], w_recv.at[j], p, peer)

    def f_copy(j):
        owner = 2 * ((chip + half - j) % half) + core
        return remote(wrows(owner), wrows(owner), f_send.at[j], f_recv.at[j], p, sib)

    f_own = remote(w_ref, wrows(me), f_send.at[0], f_recv.at[0], p, sib)

    def start_w(j, _):
        w_copy(j).start()
        return 0

    lax.fori_loop(1, half, start_w, 0)
    f_own.start()
    own_w = pltpu.make_async_copy(w_ref, wrows(me), loc.at[0])
    own_w.start()

    @pl.when(last)
    def _():
        s1r[...] = jnp.zeros_like(s1r)
        s0r[...] = jnp.zeros_like(s0r)
        for t in range(heads):
            acc = go_ref[:, t * tile:t * tile + HEAD].astype(F32)
            for r in range(1, group):
                lo = t * tile + r * HEAD
                acc = acc + go_ref[:, lo:lo + HEAD].astype(F32)
            vcur[1, :, t * HEAD:(t + 1) * HEAD] = acc.astype(BF16)

    @pl.when(first)
    def _():
        p1r[...] = jnp.zeros_like(p1r)

    for l in range(2):
        total = jnp.zeros((tok, HEAD), F32)
        for t in range(width // HEAD):
            xx = x_ref[l, :, t * HEAD:(t + 1) * HEAD].astype(F32)
            total = total + xx * xx
        mean = jnp.sum(total, axis=-1, keepdims=True) / width
        rinv[l] = jnp.broadcast_to(lax.rsqrt(mean + 1e-05), (tok, HEAD))
        for t in range(width // HEAD):
            cols = slice(t * HEAD, (t + 1) * HEAD)
            xn = x_ref[l, :, cols].astype(F32) * rinv[l]
            hid = xn * g_ref[l:l + 1, cols]
            ht[cols, l * tok:(l + 1) * tok] = hid.T.astype(BF16)

    def hrows(owner):
        return ht.at[pl.ds(pl.multiple_of(owner * shard, shard), shard)]

    wide = 2 * tok
    hslot = hall.at[:, pl.ds(pl.multiple_of(me * wide, wide), wide)]

    def h_copy(j):
        peer = (me + j) % ndp
        return remote(hrows(peer), hslot, h_send.at[j], h_recv.at[j], p, peer)

    def start_h(j, _):
        h_copy(j).start()
        return 0

    own_h = pltpu.make_async_copy(hrows(me), hslot, loc.at[1])
    own_h.start()

    def forward_w(j, _):
        w_copy(j).wait_recv()
        f_copy(j).start()
        return 0

    lax.fori_loop(1, half, forward_w, 0)
    own_w.wait()
    f_own.wait_recv()

    def arrived_w(j, _):
        f_copy(j).wait_recv()
        return 0

    lax.fori_loop(1, half, arrived_w, 0)

    def d_slot(l):
        return dvall.at[pl.ds(pl.multiple_of((me * 2 + l) * tok, tok), tok)]

    def d_copy(l, j):
        peer = (me + j) % ndp
        return remote(
            vcur.at[l], d_slot(l), d_send.at[l, j], d_recv.at[l, j], p, peer
        )

    def v_copy(l, b):
        slot = l - (npipe - 1 - p) // (npipe - 1)
        rows = pl.ds(b * brow, brow)
        return remote(
            vsend.at[l, rows], vcur.at[slot, rows],
            v_send.at[l, b], v_recv.at[slot, b], below, me,
        )

    def v_arrival(l, b):
        rows = pl.ds(b * brow, brow)
        return remote(
            vsend.at[l, rows], vcur.at[l, rows],
            v_send.at[l, b], v_recv.at[l, b], below, me,
        )

    def turn(l):
        for b in range(BLOCKS):
            rows = slice(b * brow, (b + 1) * brow)
            if l == 1:
                @pl.when(jnp.logical_not(last))
                def _():
                    v_arrival(l, b).wait_recv()
            else:
                v_arrival(l, b).wait_recv()
            vb = vcur[l, rows]
            ri = rinv[l, rows]
            total = jnp.zeros((brow, HEAD), F32)
            for t in range(heads):
                dh = lax.dot_general(
                    vb, wfull[t * tile:(t + 1) * tile],
                    (((1,), (1,)), ((), ())), preferred_element_type=F32,
                )
                for r in range(group):
                    cols = slice(t * tile + r * HEAD, t * tile + (r + 1) * HEAD)
                    d = dh[:, r * HEAD:(r + 1) * HEAD] * g_ref[l:l + 1, cols]
                    dhg[:, cols] = d
                    total = total + d * (x_ref[l, rows, cols].astype(F32) * ri)
            mean = jnp.sum(total, axis=-1, keepdims=True) / width
            for t in range(heads):
                acc = vb[:, t * HEAD:(t + 1) * HEAD].astype(F32)
                for r in range(group):
                    cols = slice(t * tile + r * HEAD, t * tile + (r + 1) * HEAD)
                    xn = x_ref[l, rows, cols].astype(F32) * ri
                    c = ri * (dhg[:, cols] - xn * mean)
                    cbuf[l, rows, cols] = c
                    acc = acc + c
                vsend[l, rows, t * HEAD:(t + 1) * HEAD] = acc.astype(BF16)
            if l == 1:
                v_copy(l, b).start()
            else:
                @pl.when(jnp.logical_not(first))
                def _():
                    v_copy(l, b).start()

        def start_d(j, _):
            d_copy(l, j).start()
            return 0

        lax.fori_loop(1, ndp, start_d, 0)
        own = pltpu.make_async_copy(vcur.at[l], d_slot(l), loc.at[2 + l])
        own.start()
        return own

    def crows(i):
        return pl.ds(pl.multiple_of(i * crow, crow), crow)

    def s1_copy(i):
        r = crows(i)
        return remote(s1s.at[r], s1r.at[r], s1_ss.at[i], s1_rs.at[i], below, me)

    def s0_copy(i):
        r = crows(i)
        return remote(s0s.at[r], s0r.at[r], s0_ss.at[i], s0_rs.at[i], below, me)

    def p1_copy(i):
        r = crows(i)
        return remote(p1s.at[r], p1r.at[r], p1_ss.at[i], p1_rs.at[i], above, me)

    def windowed(copy, i):
        @pl.when(i >= WINDOW)
        def _():
            copy(i - WINDOW).wait_send()
        copy(i).start()

    def relay_s1(i, _):
        @pl.when(jnp.logical_not(last))
        def _():
            s1_copy(i).wait_recv()
        r = crows(i)
        s1 = cbuf[1, r] + s1r[r].astype(F32)
        s1s[r] = s1.astype(BF16)

        @pl.when(jnp.logical_not(first))
        def _():
            windowed(s1_copy, i)

        @pl.when(first)
        def _():
            p1s[r] = cbuf[1, r].astype(BF16)
            windowed(p1_copy, i)
        gx_ref[1, r] = (go_ref[r].astype(F32) + s1).astype(BF16)
        return 0

    own_d1 = turn(1)
    lax.fori_loop(1, ndp, start_h, 0)

    lax.fori_loop(0, EARLY, relay_s1, 0)
    own_d0 = turn(0)
    lax.fori_loop(EARLY, CHUNKS, relay_s1, 0)

    def relay_s0(i, _):
        r = crows(i)

        @pl.when(jnp.logical_not(last))
        def _():
            s0_copy(i).wait_recv()
        s0 = cbuf[0, r] + s0r[r].astype(F32)

        @pl.when(jnp.logical_not(first))
        def _():
            s0s[r] = s0.astype(BF16)
            windowed(s0_copy, i)
        cbuf[0, r] = s0
        return 0

    def relay_p1(i, _):
        r = crows(i)

        @pl.when(jnp.logical_not(first) & jnp.logical_not(last))
        def _():
            p1_copy(i).wait_recv()
            p1s[r] = (cbuf[1, r] + p1r[r].astype(F32)).astype(BF16)
            windowed(p1_copy, i)
        return 0

    def relay_both(i, _):
        relay_p1(i + AHEAD, 0)
        return relay_s0(i, 0)

    def finish(i, _):
        r = crows(i)

        @pl.when(last)
        def _():
            p1_copy(i).wait_recv()
        dy = go_ref[r].astype(F32) + (cbuf[1, r] + s1r[r].astype(F32))
        gx_ref[0, r] = (dy + p1r[r].astype(F32) + cbuf[0, r]).astype(BF16)
        return 0

    lax.fori_loop(0, AHEAD, relay_p1, 0)
    lax.fori_loop(0, CHUNKS - AHEAD, relay_both, 0)
    lax.fori_loop(CHUNKS - AHEAD, CHUNKS, relay_s0, 0)

    def arrived_h(j, _):
        h_copy(j).wait_recv()
        d_copy(0, j).wait_recv()
        d_copy(1, j).wait_recv()
        return 0

    lax.fori_loop(1, ndp, arrived_h, 0)
    own_h.wait()
    own_d1.wait()
    own_d0.wait()
    depth = ndp * wide
    step = min(depth, 2048)

    def product(k):
        cols = pl.ds(pl.multiple_of(k * step, step), step)
        return jnp.dot(hall[:, cols], dvall[cols], preferred_element_type=F32)

    gw_ref[...] = product(0)

    def more(k, _):
        gw_ref[...] += product(k)
        return 0

    if depth > step:
        lax.fori_loop(1, depth // step, more, 0)

    lax.fori_loop(0, CHUNKS, finish, 0)

    def sent_w(j, _):
        w_copy(j).wait_send()
        f_copy(j).wait_send()
        return 0

    lax.fori_loop(1, half, sent_w, 0)
    f_own.wait_send()

    def sent_h(j, _):
        h_copy(j).wait_send()
        d_copy(0, j).wait_send()
        d_copy(1, j).wait_send()
        return 0

    lax.fori_loop(1, ndp, sent_h, 0)
    for b in range(BLOCKS):
        v_copy(1, b).wait_send()

    def sent_s(i, _):
        s1_copy(i).wait_send()
        s0_copy(i).wait_send()
        return 0

    def sent_p(i, _):
        p1_copy(i).wait_send()
        return 0

    @pl.when(jnp.logical_not(first))
    def _():
        for b in range(BLOCKS):
            v_copy(0, b).wait_send()
        lax.fori_loop(CHUNKS - WINDOW, CHUNKS, sent_s, 0)

    @pl.when(jnp.logical_not(last))
    def _():
        lax.fori_loop(CHUNKS - WINDOW, CHUNKS, sent_p, 0)


def on_device(saved, grad_out, gain, w_value):
    npipe = lax.axis_size("pipe")
    ndp = lax.axis_size("dp")
    tok, width = grad_out.shape
    shard, kv = w_value.shape[1:]
    wide = 2 * tok
    dma = pltpu.SemaphoreType.DMA
    vmem = pl.BlockSpec(memory_space=pltpu.VMEM)
    gx, gw = pl.pallas_call(
        functools.partial(kernel, npipe, ndp),
        out_shape=(
            jax.ShapeDtypeStruct((2, tok, width), BF16),
            jax.ShapeDtypeStruct((shard, kv), F32),
        ),
        in_specs=[vmem] * 4,
        out_specs=(vmem, vmem),
        scratch_shapes=[
            pltpu.VMEM((width, kv), BF16),
            pltpu.VMEM((width, wide), BF16),
            pltpu.VMEM((shard, ndp * wide), BF16),
            pltpu.VMEM((ndp * wide, kv), BF16),
            pltpu.VMEM((2, tok, kv), BF16),
            pltpu.VMEM((2, tok, kv), BF16),
            pltpu.VMEM((2, tok, width), F32),
            pltpu.VMEM((tok // BLOCKS, width), F32),
            pltpu.VMEM((2, tok, HEAD), F32),
        ]
        + [pltpu.VMEM((tok, width), BF16)] * 6
        + [dma((ndp,))] * 6
        + [dma((2, ndp))] * 2
        + [dma((2, BLOCKS))] * 2
        + [dma((CHUNKS,))] * 6
        + [dma((4,))],
        compiler_params=pltpu.CompilerParams(
            collective_id=0, has_side_effects=True, vmem_limit_bytes=60 * 1024 * 1024
        ),
    )(saved[:, 0], grad_out, gain[:, 0], w_value[0])
    return gx[:, None], gw[None]


def solution(mesh):
    return jax.shard_map(
        on_device,
        mesh=mesh,
        in_specs=(
            P(None, "pipe", "dp", None),
            P("dp", None),
            P(None, "pipe", None),
            P("pipe", "dp", None),
        ),
        out_specs=(P(None, "pipe", "dp", None), P("pipe", "dp", None)),
        check_vma=False,
    )
```

```python
import functools

import jax
import jax.numpy as jnp
from jax import lax
from jax.experimental import pallas as pl
from jax.experimental.pallas import tpu as pltpu
from jax.sharding import PartitionSpec as P

HEAD = 128
BLOCKS = 2
CHUNKS = 8
EARLY = 2
WINDOW = 2
AHEAD = 3
MESH = pl.DeviceIdType.MESH
F32 = jnp.float32
BF16 = jnp.bfloat16


def kernel(
    npipe, ndp,
    x_ref, go_ref, g_ref, w_ref, gx_ref, gw_ref,
    wfull, ht, hall, dvall, vcur, vsend, cbuf, dhg, rinv,
    s1r, s0r, p1r, s1s, s0s, p1s,
    w_send, w_recv, f_send, f_recv, h_send, h_recv, d_send, d_recv,
    v_send, v_recv, s1_ss, s1_rs, s0_ss, s0_rs, p1_ss, p1_rs, loc,
):
    p = lax.axis_index("pipe")
    me = lax.axis_index("dp")
    tok, width = go_ref.shape
    kv = w_ref.shape[1]
    shard = w_ref.shape[0]
    group = width // kv
    tile = group * HEAD
    heads = kv // HEAD
    half = ndp // 2
    chip = me // 2
    core = me % 2
    sib = 2 * chip + 1 - core
    below = (p + npipe - 1) % npipe
    above = (p + 1) % npipe
    brow = tok // BLOCKS
    crow = tok // CHUNKS
    last = p == npipe - 1
    first = p == 0

    def remote(src, dst, ss, rs, pipe, dp):
        return pltpu.make_async_remote_copy(
            src_ref=src, dst_ref=dst, send_sem=ss, recv_sem=rs,
            device_id=(pipe, dp), device_id_type=MESH,
        )

    barrier = pltpu.get_barrier_semaphore()

    def greet(j, _):
        pl.semaphore_signal(
            barrier, inc=1, device_id=(p, (me + j) % ndp), device_id_type=MESH
        )
        return 0

    lax.fori_loop(1, ndp, greet, 0)
    pl.semaphore_signal(barrier, inc=1, device_id=(below, me), device_id_type=MESH)
    pl.semaphore_signal(barrier, inc=1, device_id=(above, me), device_id_type=MESH)
    pl.semaphore_wait(barrier, ndp + 1)

    def wrows(owner):
        return wfull.at[pl.ds(pl.multiple_of(owner * shard, shard), shard)]

    def w_copy(j):
        peer = 2 * ((chip + j) % half) + core
        return remote(w_ref, wrows(me), w_send.at[j], w_recv.at[j], p, peer)

    def f_copy(j):
        owner = 2 * ((chip + half - j) % half) + core
        return remote(wrows(owner), wrows(owner), f_send.at[j], f_recv.at[j], p, sib)

    f_own = remote(w_ref, wrows(me), f_send.at[0], f_recv.at[0], p, sib)

    def start_w(j, _):
        w_copy(j).start()
        return 0

    lax.fori_loop(1, half, start_w, 0)
    f_own.start()
    own_w = pltpu.make_async_copy(w_ref, wrows(me), loc.at[0])
    own_w.start()

    @pl.when(last)
    def _():
        s1r[...] = jnp.zeros_like(s1r)
        s0r[...] = jnp.zeros_like(s0r)
        for t in range(heads):
            acc = go_ref[:, t * tile:t * tile + HEAD].astype(F32)
            for r in range(1, group):
                lo = t * tile + r * HEAD
                acc = acc + go_ref[:, lo:lo + HEAD].astype(F32)
            vcur[1, :, t * HEAD:(t + 1) * HEAD] = acc.astype(BF16)

    @pl.when(first)
    def _():
        p1r[...] = jnp.zeros_like(p1r)

    for l in range(2):
        total = jnp.zeros((tok, HEAD), F32)
        for t in range(width // HEAD):
            xx = x_ref[l, :, t * HEAD:(t + 1) * HEAD].astype(F32)
            total = total + xx * xx
        mean = jnp.sum(total, axis=-1, keepdims=True) / width
        rinv[l] = jnp.broadcast_to(lax.rsqrt(mean + 1e-05), (tok, HEAD))
        for t in range(width // HEAD):
            cols = slice(t * HEAD, (t + 1) * HEAD)
            xn = x_ref[l, :, cols].astype(F32) * rinv[l]
            hid = xn * g_ref[l:l + 1, cols]
            ht[cols, l * tok:(l + 1) * tok] = hid.T.astype(BF16)

    def hrows(owner):
        return ht.at[pl.ds(pl.multiple_of(owner * shard, shard), shard)]

    wide = 2 * tok
    hslot = hall.at[:, pl.ds(pl.multiple_of(me * wide, wide), wide)]

    def h_copy(j):
        peer = (me + j) % ndp
        return remote(hrows(peer), hslot, h_send.at[j], h_recv.at[j], p, peer)

    def start_h(j, _):
        h_copy(j).start()
        return 0

    own_h = pltpu.make_async_copy(hrows(me), hslot, loc.at[1])
    own_h.start()

    def forward_w(j, _):
        w_copy(j).wait_recv()
        f_copy(j).start()
        return 0

    lax.fori_loop(1, half, forward_w, 0)
    own_w.wait()
    f_own.wait_recv()

    def arrived_w(j, _):
        f_copy(j).wait_recv()
        return 0

    lax.fori_loop(1, half, arrived_w, 0)

    def d_slot(l):
        return dvall.at[pl.ds(pl.multiple_of((me * 2 + l) * tok, tok), tok)]

    def d_copy(l, j):
        peer = (me + j) % ndp
        return remote(
            vcur.at[l], d_slot(l), d_send.at[l, j], d_recv.at[l, j], p, peer
        )

    def v_copy(l, b):
        slot = l - (npipe - 1 - p) // (npipe - 1)
        rows = pl.ds(b * brow, brow)
        return remote(
            vsend.at[l, rows], vcur.at[slot, rows],
            v_send.at[l, b], v_recv.at[slot, b], below, me,
        )

    def v_arrival(l, b):
        rows = pl.ds(b * brow, brow)
        return remote(
            vsend.at[l, rows], vcur.at[l, rows],
            v_send.at[l, b], v_recv.at[l, b], below, me,
        )

    def turn(l):
        for b in range(BLOCKS):
            rows = slice(b * brow, (b + 1) * brow)
            if l == 1:
                @pl.when(jnp.logical_not(last))
                def _():
                    v_arrival(l, b).wait_recv()
            else:
                v_arrival(l, b).wait_recv()
            vb = vcur[l, rows]
            ri = rinv[l, rows]
            total = jnp.zeros((brow, HEAD), F32)
            for t in range(heads):
                dh = lax.dot_general(
                    vb, wfull[t * tile:(t + 1) * tile],
                    (((1,), (1,)), ((), ())), preferred_element_type=F32,
                )
                for r in range(group):
                    cols = slice(t * tile + r * HEAD, t * tile + (r + 1) * HEAD)
                    d = dh[:, r * HEAD:(r + 1) * HEAD] * g_ref[l:l + 1, cols]
                    dhg[:, cols] = d
                    total = total + d * (x_ref[l, rows, cols].astype(F32) * ri)
            mean = jnp.sum(total, axis=-1, keepdims=True) / width
            for t in range(heads):
                acc = vb[:, t * HEAD:(t + 1) * HEAD].astype(F32)
                for r in range(group):
                    cols = slice(t * tile + r * HEAD, t * tile + (r + 1) * HEAD)
                    xn = x_ref[l, rows, cols].astype(F32) * ri
                    c = ri * (dhg[:, cols] - xn * mean)
                    cbuf[l, rows, cols] = c
                    acc = acc + c
                vsend[l, rows, t * HEAD:(t + 1) * HEAD] = acc.astype(BF16)
            if l == 1:
                v_copy(l, b).start()
            else:
                @pl.when(jnp.logical_not(first))
                def _():
                    v_copy(l, b).start()

        def start_d(j, _):
            d_copy(l, j).start()
            return 0

        lax.fori_loop(1, ndp, start_d, 0)
        own = pltpu.make_async_copy(vcur.at[l], d_slot(l), loc.at[2 + l])
        own.start()
        return own

    def crows(i):
        return pl.ds(pl.multiple_of(i * crow, crow), crow)

    def s1_copy(i):
        r = crows(i)
        return remote(s1s.at[r], s1r.at[r], s1_ss.at[i], s1_rs.at[i], below, me)

    def s0_copy(i):
        r = crows(i)
        return remote(s0s.at[r], s0r.at[r], s0_ss.at[i], s0_rs.at[i], below, me)

    def p1_copy(i):
        r = crows(i)
        return remote(p1s.at[r], p1r.at[r], p1_ss.at[i], p1_rs.at[i], above, me)

    def windowed(copy, i):
        @pl.when(i >= WINDOW)
        def _():
            copy(i - WINDOW).wait_send()
        copy(i).start()

    def relay_s1(i, _):
        @pl.when(jnp.logical_not(last))
        def _():
            s1_copy(i).wait_recv()
        r = crows(i)
        s1 = cbuf[1, r] + s1r[r].astype(F32)
        s1s[r] = s1.astype(BF16)

        @pl.when(jnp.logical_not(first))
        def _():
            windowed(s1_copy, i)

        @pl.when(first)
        def _():
            p1s[r] = cbuf[1, r].astype(BF16)
            windowed(p1_copy, i)
        gx_ref[1, r] = (go_ref[r].astype(F32) + s1).astype(BF16)
        return 0

    own_d1 = turn(1)
    lax.fori_loop(1, ndp, start_h, 0)

    lax.fori_loop(0, EARLY, relay_s1, 0)
    own_d0 = turn(0)
    lax.fori_loop(EARLY, CHUNKS, relay_s1, 0)

    def relay_s0(i, _):
        r = crows(i)

        @pl.when(jnp.logical_not(last))
        def _():
            s0_copy(i).wait_recv()
        s0 = cbuf[0, r] + s0r[r].astype(F32)

        @pl.when(jnp.logical_not(first))
        def _():
            s0s[r] = s0.astype(BF16)
            windowed(s0_copy, i)
        cbuf[0, r] = s0
        return 0

    def relay_p1(i, _):
        r = crows(i)

        @pl.when(jnp.logical_not(first) & jnp.logical_not(last))
        def _():
            p1_copy(i).wait_recv()
            p1s[r] = (cbuf[1, r] + p1r[r].astype(F32)).astype(BF16)
            windowed(p1_copy, i)
        return 0

    def relay_both(i, _):
        relay_p1(i + AHEAD, 0)
        return relay_s0(i, 0)

    def finish(i, _):
        r = crows(i)

        @pl.when(last)
        def _():
            p1_copy(i).wait_recv()
        dy = go_ref[r].astype(F32) + (cbuf[1, r] + s1r[r].astype(F32))
        gx_ref[0, r] = (dy + p1r[r].astype(F32) + cbuf[0, r]).astype(BF16)
        return 0

    lax.fori_loop(0, AHEAD, relay_p1, 0)
    lax.fori_loop(0, CHUNKS - AHEAD, relay_both, 0)
    lax.fori_loop(CHUNKS - AHEAD, CHUNKS, relay_s0, 0)

    def arrived_h(j, _):
        h_copy(j).wait_recv()
        d_copy(0, j).wait_recv()
        d_copy(1, j).wait_recv()
        return 0

    lax.fori_loop(1, ndp, arrived_h, 0)
    own_h.wait()
    own_d1.wait()
    own_d0.wait()
    depth = ndp * wide
    step = min(depth, 2048)

    def product(k):
        cols = pl.ds(pl.multiple_of(k * step, step), step)
        return jnp.dot(hall[:, cols], dvall[cols], preferred_element_type=F32)

    gw_ref[...] = product(0)

    def more(k, _):
        gw_ref[...] += product(k)
        return 0

    if depth > step:
        lax.fori_loop(1, depth // step, more, 0)

    lax.fori_loop(0, CHUNKS, finish, 0)

    def sent_w(j, _):
        w_copy(j).wait_send()
        f_copy(j).wait_send()
        return 0

    lax.fori_loop(1, half, sent_w, 0)
    f_own.wait_send()

    def sent_h(j, _):
        h_copy(j).wait_send()
        d_copy(0, j).wait_send()
        d_copy(1, j).wait_send()
        return 0

    lax.fori_loop(1, ndp, sent_h, 0)
    for b in range(BLOCKS):
        v_copy(1, b).wait_send()

    def sent_s(i, _):
        s1_copy(i).wait_send()
        s0_copy(i).wait_send()
        return 0

    def sent_p(i, _):
        p1_copy(i).wait_send()
        return 0

    @pl.when(jnp.logical_not(first))
    def _():
        for b in range(BLOCKS):
            v_copy(0, b).wait_send()
        lax.fori_loop(CHUNKS - WINDOW, CHUNKS, sent_s, 0)

    @pl.when(jnp.logical_not(last))
    def _():
        lax.fori_loop(CHUNKS - WINDOW, CHUNKS, sent_p, 0)


def on_device(saved, grad_out, gain, w_value):
    npipe = lax.axis_size("pipe")
    ndp = lax.axis_size("dp")
    tok, width = grad_out.shape
    shard, kv = w_value.shape[1:]
    wide = 2 * tok
    dma = pltpu.SemaphoreType.DMA
    vmem = pl.BlockSpec(memory_space=pltpu.VMEM)
    gx, gw = pl.pallas_call(
        functools.partial(kernel, npipe, ndp),
        out_shape=(
            jax.ShapeDtypeStruct((2, tok, width), BF16),
            jax.ShapeDtypeStruct((shard, kv), F32),
        ),
        in_specs=[vmem] * 4,
        out_specs=(vmem, vmem),
        scratch_shapes=[
            pltpu.VMEM((width, kv), BF16),
            pltpu.VMEM((width, wide), BF16),
            pltpu.VMEM((shard, ndp * wide), BF16),
            pltpu.VMEM((ndp * wide, kv), BF16),
            pltpu.VMEM((2, tok, kv), BF16),
            pltpu.VMEM((2, tok, kv), BF16),
            pltpu.VMEM((2, tok, width), F32),
            pltpu.VMEM((tok // BLOCKS, width), F32),
            pltpu.VMEM((2, tok, HEAD), F32),
        ]
        + [pltpu.VMEM((tok, width), BF16)] * 6
        + [dma((ndp,))] * 6
        + [dma((2, ndp))] * 2
        + [dma((2, BLOCKS))] * 2
        + [dma((CHUNKS,))] * 6
        + [dma((4,))],
        compiler_params=pltpu.CompilerParams(
            collective_id=0, has_side_effects=True, vmem_limit_bytes=60 * 1024 * 1024
        ),
    )(saved[:, 0], grad_out, gain[:, 0], w_value[0])
    return gx[:, None], gw[None]


def solution(mesh):
    return jax.shard_map(
        on_device,
        mesh=mesh,
        in_specs=(
            P(None, "pipe", "dp", None),
            P("dp", None),
            P(None, "pipe", None),
            P("pipe", "dp", None),
        ),
        out_specs=(P(None, "pipe", "dp", None), P("pipe", "dp", None)),
        check_vma=False,
    )
```
